32 devices in a mesh: epoch: 4 (over x, core), row: 8 (over z, y).
Axes of the slice: x: 2, y: 2, z: 4, core: 2. Of those that a mesh axis runs over, the one named last changes fastest.
Arguments:
- flux_image: float32 [16, 256, 1024], P('epoch', 'row'), may hold values from -8 to 8
- inv_var: float32 [16, 256, 1024], P('epoch', 'row'), may hold values from 0.5 to 4
- pixel_mask: int32 [16, 256, 1024], P('epoch', 'row'), may hold values 0 or 1
- psf_columns: float32 [16, 13], P('epoch'), may hold values from 0.02 to 0.3
- psf_rows: float32 [16, 13], P('epoch'), may hold values from 0.02 to 0.3
- epoch_times: int32 [16], P('epoch'), may hold values from 0 to 63, as said below
- trial_rates: int32 [4, 2], replicated, may hold values from -8 to 8, as said below
Outputs:
- psi_stack: float32 [4, 256, 1024], P('epoch', 'row')
- phi_stack: float32 [4, 256, 1024], P('epoch', 'row')
The draws below stay inside these ranges and needn't reach their ends.
Inputs may be any that keep to these rules, and one draw needn't show every extreme that they name: `epoch_times`: some epoch has time index 0 and some has 63. `trial_rates`: some velocity has row rate 8 and some -8; some has column rate 8 and some -8.
All inputs are finite; a program needn't handle non-finite values. No bound on the sum of `pixel_mask` on one device may be relied on, other than what follows from the above.
Results may differ from the reference program's by a relative error of at most 0.00011.
Values sent between devices are 32-bit elements; how exact they have to be, the bound alone decides.
A program may use at most 64 MiB of HBM per device.

```python
import math
import jax
import jax.numpy as jnp
from jax import lax

COLS = 1024
HALO = 8
PAD = 6
TSPAN = 64
KW = 13
EPOCHS = 16
VELS = 4
ROWS = 256


def draw_epoch_times(key, part):
    base_key, pick_key = jax.random.split(jax.random.fold_in(key, 11))
    values = jax.random.randint(base_key, (EPOCHS,), 0, TSPAN, dtype=jnp.int32)
    order = jax.random.permutation(pick_key, EPOCHS)
    return values.at[order[0]].set(0).at[order[1]].set(TSPAN - 1)


def draw_trial_rates(key, part):
    base_key, pick_key = jax.random.split(jax.random.fold_in(key, 23))
    values = jax.random.randint(base_key, (VELS, 2), -HALO, HALO + 1, dtype=jnp.int32)
    order = jax.random.permutation(pick_key, VELS)
    values = values.at[order[0], 0].set(HALO).at[order[1], 0].set(-HALO)
    return values.at[order[2], 1].set(HALO).at[order[3], 1].set(-HALO)


def with_ends(array, stream_key, low, top_value):
    extent = array.shape
    index_at = [jax.random.randint(jax.random.fold_in(stream_key, axis), (), 0, extent[axis]) for axis in range(len(extent))]
    array = array.at[tuple(index_at)].set(low)
    longest = extent.index(max(extent))
    index_at[longest] = (index_at[longest] + 1) % extent[longest]
    return array.at[tuple(index_at)].set(top_value)


def block_levels(own_key, extent, pieces, smallest, largest):
    def one(dim, blocks):
        heights = jax.random.uniform(jax.random.fold_in(jax.random.fold_in(own_key, 6), dim), (blocks,), jnp.float32, smallest / len(pieces), largest / len(pieces))
        return jnp.repeat(jnp.exp(heights), extent[dim] // blocks).reshape((-1,) + (1,) * (len(extent) - dim - 1))

    loudness = one(*pieces[0])
    for cut in pieces[1:]:
        loudness = loudness * one(*cut)
    return loudness


def normal_values(own_key, shape, width, reach, pieces=(), kind=jnp.bfloat16):
    entries = width * jax.random.normal(own_key, shape, jnp.float32)
    if pieces:
        entries = entries * block_levels(own_key, shape, pieces, -0.22, 0.18)
    return jnp.clip(entries, -reach, reach).astype(kind)


def setup_inputs(seed: int = 0) -> dict:
    key_of = jax.random.split(jax.random.key(seed), 8)
    flux_image = normal_values(key_of[0], (EPOCHS, ROWS, COLS), 1.0, 8.0, ((0, 4), (1, 8)), jnp.float32)
    inv_var = jnp.clip(jnp.exp(math.log(4.0) - 2.0794415 * jax.random.uniform(key_of[1], (EPOCHS, ROWS, COLS), jnp.float32) ** block_levels(key_of[1], (EPOCHS, ROWS, COLS), ((0, 4), (1, 8)), -0.2, 0.2)), 0.5, 4.0)
    pixel_mask = with_ends((jax.random.randint(key_of[2], (EPOCHS, ROWS, COLS), 0, 16) < 15).astype(jnp.int32), jax.random.fold_in(key_of[2], 1), 0, 1)
    psf_columns = jnp.clip(jnp.exp(math.log(0.3) - 2.7080503 * jax.random.uniform(key_of[3], (EPOCHS, KW), jnp.float32) ** block_levels(key_of[3], (EPOCHS, KW), ((0, 4),), -0.2, 0.2)), 0.02, 0.3)
    psf_rows = jnp.clip(jnp.exp(math.log(0.3) - 2.7080503 * jax.random.uniform(key_of[4], (EPOCHS, KW), jnp.float32) ** block_levels(key_of[4], (EPOCHS, KW), ((0, 4),), -0.2, 0.2)), 0.02, 0.3)
    epoch_times = draw_epoch_times(jax.random.fold_in(key_of[7], 71), 0)
    trial_rates = draw_trial_rates(jax.random.fold_in(key_of[7], 71), 0)
    return dict(flux_image=flux_image, inv_var=inv_var, pixel_mask=pixel_mask, psf_columns=psf_columns, psf_rows=psf_rows, epoch_times=epoch_times, trial_rates=trial_rates)


def conv_columns(fields_in, kernel):
    columns = fields_in.shape[3]
    padded = jnp.pad(fields_in, ((0, 0), (0, 0), (0, 0), (PAD, PAD)))
    result = jnp.zeros(fields_in.shape, jnp.float32)
    for tap_index in range(2 * PAD + 1):
        result = result + kernel[:, :, tap_index][:, :, None, None] * padded[:, :, :, tap_index:tap_index + columns]
    return result


def conv_rows_valid(fields_in, kernel):
    out_rows = fields_in.shape[2] - 2 * PAD
    shape_out = (fields_in.shape[0], fields_in.shape[1], out_rows, fields_in.shape[3])
    result = jnp.zeros(shape_out, jnp.float32)
    for tap_index in range(2 * PAD + 1):
        result = result + kernel[:, :, tap_index][:, :, None, None] * fields_in[:, :, tap_index:tap_index + out_rows, :]
    return result


def shifted_sum(padded, row_starts, column_starts, first_vel, how_many, out_rows):
    columns = padded.shape[3] - 2 * HALO
    row_part = lax.dynamic_slice_in_dim(row_starts, first_vel, how_many, 1)
    column_part = lax.dynamic_slice_in_dim(column_starts, first_vel, how_many, 1)

    def add_epoch(epoch_number, running):
        epoch_field = lax.dynamic_index_in_dim(padded, epoch_number, 0, keepdims=False)
        row_now = lax.dynamic_index_in_dim(row_part, epoch_number, 0, keepdims=False)
        column_now = lax.dynamic_index_in_dim(column_part, epoch_number, 0, keepdims=False)

        def take_window(row_begin, column_begin):
            return lax.dynamic_slice(epoch_field, (jnp.int32(0), row_begin, column_begin), (2, out_rows, columns))

        return running + jax.vmap(take_window)(row_now, column_now)

    empty_stack = jnp.zeros((how_many, 2, out_rows, columns), jnp.float32)
    return lax.fori_loop(0, padded.shape[0], add_epoch, empty_stack)


def reference(flux_image, inv_var, pixel_mask, psf_columns, psf_rows, epoch_times, trial_rates):
    weights = inv_var * pixel_mask.astype(jnp.float32)
    fields = jnp.stack([flux_image * weights, weights], axis=1)
    fields = conv_columns(fields, jnp.stack([psf_columns, psf_columns * psf_columns], axis=1))
    row_kernel = jnp.stack([psf_rows, psf_rows * psf_rows], axis=1)
    fields = jnp.pad(fields, ((0, 0), (0, 0), (PAD, PAD), (0, 0)))
    fields = conv_rows_valid(fields, row_kernel)
    padded = jnp.pad(fields, ((0, 0), (0, 0), (HALO, HALO), (HALO, HALO)))
    row_shift = jnp.floor_divide(trial_rates[:, 0][None, :] * epoch_times[:, None], TSPAN).astype(jnp.int32)
    column_shift = jnp.floor_divide(trial_rates[:, 1][None, :] * epoch_times[:, None], TSPAN).astype(jnp.int32)
    stacks = shifted_sum(padded, row_shift + HALO, column_shift + HALO, 0, VELS, ROWS)
    return stacks[:, 0], stacks[:, 1]
```

```python
import functools

import jax
import jax.numpy as jnp
from jax import lax
from jax.experimental import pallas as pl
from jax.experimental.pallas import tpu as pltpu
from jax.sharding import PartitionSpec as P

HALO = 8
PAD = 6
TSPAN = 64
TAPS = 2 * PAD + 1
LANES = 128
NEAR = 8
OVER = 3 * NEAR
BAND = 2 * LANES
TALL = BAND + 2 * HALO
MESH = pl.DeviceIdType.MESH
F32 = jnp.float32
BF16 = jnp.bfloat16


def split(x):
    high = x.astype(BF16)
    return high, (x - high.astype(F32)).astype(BF16)


def iota(shape, axis):
    return lax.broadcasted_iota(jnp.int32, shape, axis)


def kernel(
    sizes,
    flux_hbm, inv_hbm, mask_hbm, psf_columns, psf_rows, times, rates,
    out_psi, out_phi,
    flux, inv, mask, toeplitz, padded, shifted,
    pair_out_over, pair_out_mid, pair_in_over, pair_in_mid,
    own_over, own_mid, far_in_over, far_in_mid,
    up_out, down_out, up_in, down_in,
    load_sem, pair_send, pair_recv, far_send, far_recv, row_send, row_recv,
):
    groups, row_devices = sizes
    epochs, rows, columns = flux.shape
    tiles = columns // LANES
    depth = epochs * rows
    me = lax.axis_index("epoch")
    core, group = lax.rem(me, 2), me // 2
    partner = me + 1 - 2 * core
    row = lax.axis_index("row")
    outs = (out_psi, out_phi)

    loads = []
    for e in range(epochs):
        for n, (src, dst) in enumerate(((inv_hbm, inv), (mask_hbm, mask), (flux_hbm, flux))):
            copy = pltpu.make_async_copy(src.at[e], dst.at[e], load_sem.at[e, n])
            copy.start()
            loads.append(copy)

    barrier = pltpu.get_barrier_semaphore()
    pl.semaphore_signal(barrier, inc=1, device_id={"epoch": partner}, device_id_type=MESH)
    for d in range(1, groups):
        there = 2 * lax.rem(group + d, groups) + core
        pl.semaphore_signal(barrier, inc=1, device_id={"epoch": there}, device_id_type=MESH)

    @pl.when(row > 0)
    def _():
        pl.semaphore_signal(barrier, inc=1, device_id={"row": row - 1}, device_id_type=MESH)

    @pl.when(row < row_devices - 1)
    def _():
        pl.semaphore_signal(barrier, inc=1, device_id={"row": row + 1}, device_id_type=MESH)

    offset = BAND // 4 - PAD + HALO
    lane = iota((NEAR, LANES), 1)
    place = iota((NEAR, LANES), 0) - lane
    wrapped = lax.rem(place - offset + 4 * LANES, LANES)
    for e in range(epochs):
        plain = jnp.zeros((NEAR, LANES), F32)
        for tap in range(TAPS):
            plain = jnp.where(wrapped == tap, psf_columns[e, tap], plain)
        for m in range(TALL // NEAR):
            turned = pltpu.roll(plain, (NEAR * m) % LANES, 1) if (NEAR * m) % LANES else plain
            where = place + (NEAR * m - offset)
            turned = jnp.where((where >= 0) & (where < TAPS), turned, 0.0)
            toeplitz[e, 0, m * NEAR : (m + 1) * NEAR, :] = turned
            toeplitz[e, 1, m * NEAR : (m + 1) * NEAR, :] = turned * turned

    half_lane = iota((rows, LANES), 1) < LANES // 2
    for e in range(epochs):
        for copy in loads[3 * e : 3 * e + 3]:
            copy.wait()
        weights = inv[e] * mask[e].astype(F32)
        for f, field in enumerate((flux[e] * weights, weights)):
            turned = pltpu.roll(field, LANES // 2, 1)
            first = turned[:, :LANES]
            for n, piece in enumerate(split(turned)):
                padded[e, f, n, :, LANES:columns] = piece[:, LANES:]
            for n, piece in enumerate(split(jnp.where(half_lane, 0.0, first))):
                padded[e, f, n, :, :LANES] = piece
            for n, piece in enumerate(split(jnp.where(half_lane, first, 0.0))):
                padded[e, f, n, :, columns:] = piece

    def shift(v, axis, e):
        return (rates[v, axis] * times[e]) >> (TSPAN.bit_length() - 1)

    def row_matrices(v):
        shape = (OVER + rows + NEAR, depth)
        o, k = iota(shape, 0), iota(shape, 1)
        far = jnp.where(rates[v, 0] >= 0, -2 * NEAR, rows + NEAR)
        r = jnp.where(o < NEAR, o - NEAR, rows + o - NEAR)
        r = jnp.where(o >= 2 * NEAR, o - 2 * NEAR + far, r)
        r = jnp.where(o >= OVER, o - OVER, r)
        epoch_of = k // rows
        step = jnp.zeros(shape, jnp.int32)
        for e in range(epochs):
            step = jnp.where(epoch_of == e, shift(v, 0, e), step)
        at = r + step
        good = (at + row * rows >= 0) & (at + row * rows < rows * row_devices) & (o < OVER + rows)
        tap_at = jnp.where(good, lax.rem(k, rows) - at + PAD, -1)
        one_row = epoch_of[:1]
        plain = jnp.zeros(shape, F32)
        for tap in range(TAPS):
            value = jnp.zeros((1, depth), F32)
            for e in range(epochs):
                value = jnp.where(one_row == e, psf_rows[e, tap], value)
            plain = jnp.where(tap_at == tap, value, plain)
        return split(plain), split(plain * plain)

    def columns_stage(pair, f):
        lanes = iota((rows, 2 * LANES), 1)
        for e in range(epochs):
            steps = [shift(v, 1, e) for v in pair]
            band = jnp.concatenate(
                [toeplitz[e, f, pl.ds(HALO - s, BAND), :] for s in steps], axis=1
            )
            band_high, band_low = split(band)
            high, low = (
                jnp.concatenate(
                    [padded[e, f, n, :, t * LANES : t * LANES + BAND] for t in range(tiles)], axis=0
                )
                for n in range(2)
            )
            result = jnp.dot(
                jnp.concatenate([high, low, high], axis=1),
                jnp.concatenate([band_high, band_high, band_low], axis=0),
                preferred_element_type=F32,
            )
            source = lax.rem(lanes, LANES) + jnp.where(lanes < LANES, steps[0], steps[1])
            for t in range(tiles):
                block = result[t * rows : (t + 1) * rows]
                if t == 0:
                    block = jnp.where(source >= 0, block, 0.0)
                if t == tiles - 1:
                    block = jnp.where(source + t * LANES < columns, block, 0.0)
                high_block, low_block = split(block)
                for h in range(2):
                    at = slice(t * LANES, (t + 1) * LANES)
                    part = slice(h * LANES, (h + 1) * LANES)
                    shifted[h, e * rows : (e + 1) * rows, at] = high_block[:, part]
                    shifted[h, depth + e * rows : depth + (e + 1) * rows, at] = low_block[:, part]

    def rows_stage(h, matrix):
        high, low = matrix
        return jnp.dot(
            jnp.concatenate([high, high], axis=1), shifted[h], preferred_element_type=F32
        ) + jnp.dot(low, shifted[h, :depth], preferred_element_type=F32)

    def pair_copy(d, f, part):
        src, dst = ((pair_out_over, pair_in_over), (pair_out_mid, pair_in_mid))[part]
        return pltpu.make_async_remote_copy(
            src_ref=src.at[d, f], dst_ref=dst.at[d, f],
            send_sem=pair_send.at[d, f, part], recv_sem=pair_recv.at[d, f, part],
            device_id={"epoch": partner}, device_id_type=MESH,
        )

    def far_copy(d, f, part):
        src, dst = ((own_over, far_in_over), (own_mid, far_in_mid))[part]
        return pltpu.make_async_remote_copy(
            src_ref=src.at[d, f], dst_ref=dst.at[d - 1, f],
            send_sem=far_send.at[d - 1, f, part], recv_sem=far_recv.at[d - 1, f, part],
            device_id={"epoch": 2 * lax.rem(group + d, groups) + core}, device_id_type=MESH,
        )

    def row_copy(f, way, other):
        src, dst = ((up_out, down_in), (down_out, up_in))[way]
        return pltpu.make_async_remote_copy(
            src_ref=src.at[f], dst_ref=dst.at[f],
            send_sem=row_send.at[f, way], recv_sem=row_recv.at[f, way],
            device_id={"row": other}, device_id_type=MESH,
        )

    def finish(d, f):
        for part, (own, arrived) in enumerate(((own_over, pair_in_over), (own_mid, pair_in_mid))):
            pair_copy(d, f, part).wait_recv()
            own[d, f] = own[d, f] + arrived[d, f]
            if d:
                far_copy(d, f, part).start()

    order = list(range(1, groups)) + [0]
    before = None
    for d in order:
        goal = 2 * lax.rem(group + d, groups)
        pair = (goal + 1 - core, goal + core)
        matrices = [row_matrices(v) for v in pair]
        for f in range(2):
            columns_stage(pair, f)
            if before is None:
                above = lax.div(row + row_devices - 1, row_devices)
                below = lax.div(2 * row_devices - 2 - row, row_devices)
                pl.semaphore_wait(barrier, groups + above + below)
            else:
                finish(*before)
            part = rows_stage(0, matrices[0][f])
            pair_out_over[d, f] = part[:OVER]
            pair_out_mid[d, f] = part[OVER : OVER + rows]
            pair_copy(d, f, 0).start()
            pair_copy(d, f, 1).start()
            part = rows_stage(1, matrices[1][f])
            own_over[d, f] = part[:OVER]
            own_mid[d, f] = part[OVER : OVER + rows]
            before = (d, f)
    finish(*before)

    upward = rates[me, 0] >= 0
    for f in range(2):
        total = own_over[0, f]
        for d in range(1, groups):
            far_copy(d, f, 0).wait_recv()
            total = total + far_in_over[d - 1, f]
        far = total[2 * NEAR :]
        up_out[f, :NEAR] = jnp.where(upward, far, 0.0)
        up_out[f, NEAR:] = total[:NEAR]
        down_out[f, :NEAR] = total[NEAR : 2 * NEAR]
        down_out[f, NEAR:] = jnp.where(upward, 0.0, far)

        @pl.when(row > 0)
        def _():
            row_copy(f, 0, row - 1).start()

        @pl.when(row < row_devices - 1)
        def _():
            row_copy(f, 1, row + 1).start()

        total = own_mid[0, f]
        for d in range(1, groups):
            far_copy(d, f, 1).wait_recv()
            total = total + far_in_mid[d - 1, f]
        outs[f][0] = total

    for f in range(2):
        @pl.when(row > 0)
        def _():
            row_copy(f, 1, row - 1).wait_recv()
            outs[f][0, : 2 * NEAR] = outs[f][0, : 2 * NEAR] + up_in[f]

        @pl.when(row < row_devices - 1)
        def _():
            row_copy(f, 0, row + 1).wait_recv()
            outs[f][0, rows - 2 * NEAR :] = outs[f][0, rows - 2 * NEAR :] + down_in[f]

    for f in range(2):
        for part in range(2):
            for d in range(groups):
                pair_copy(d, f, part).wait_send()
            for d in range(1, groups):
                far_copy(d, f, part).wait_send()

        @pl.when(row > 0)
        def _():
            row_copy(f, 0, row - 1).wait_send()

        @pl.when(row < row_devices - 1)
        def _():
            row_copy(f, 1, row + 1).wait_send()


def solution(mesh):
    epoch_devices, row_devices = mesh.shape["epoch"], mesh.shape["row"]
    groups = epoch_devices // 2

    def on_device(flux_image, inv_var, pixel_mask, psf_columns, psf_rows, epoch_times, trial_rates):
        epochs, rows, columns = flux_image.shape
        depth = epochs * rows
        assert epoch_devices % 2 == 0 and trial_rates.shape[0] == epoch_devices
        assert rows % (2 * NEAR) == 0 and columns % LANES == 0 and depth % LANES == 0
        far = max(groups - 1, 1)
        hbm = pl.BlockSpec(memory_space=pl.ANY)
        smem = pl.BlockSpec(memory_space=pltpu.SMEM)
        vmem = pl.BlockSpec(memory_space=pltpu.VMEM)
        image = (epochs, rows, columns)

        def pieces(count):
            return [
                pltpu.VMEM((count, 2, OVER, columns), F32),
                pltpu.VMEM((count, 2, rows, columns), F32),
            ]

        edge = pltpu.VMEM((2, 2 * NEAR, columns), F32)
        dma = pltpu.SemaphoreType.DMA
        return tuple(pl.pallas_call(
            functools.partial(kernel, (groups, row_devices)),
            out_shape=[jax.ShapeDtypeStruct((1, rows, columns), F32)] * 2,
            in_specs=[hbm] * 3 + [smem] * 4,
            out_specs=[vmem] * 2,
            scratch_shapes=[
                pltpu.VMEM(image, F32),
                pltpu.VMEM(image, F32),
                pltpu.VMEM(image, jnp.int32),
                pltpu.VMEM((epochs, 2, TALL, LANES), F32),
                pltpu.VMEM((epochs, 2, 2, rows, columns + LANES), BF16),
                pltpu.VMEM((2, 2 * depth, columns), BF16),
                *pieces(groups),
                *pieces(groups),
                *pieces(groups),
                *pieces(far),
                edge, edge, edge, edge,
                dma((epochs, 3)),
                dma((groups, 2, 2)),
                dma((groups, 2, 2)),
                dma((far, 2, 2)),
                dma((far, 2, 2)),
                dma((2, 2)),
                dma((2, 2)),
            ],
            compiler_params=pltpu.CompilerParams(collective_id=0, has_side_effects=True),
        )(flux_image, inv_var, pixel_mask, psf_columns, psf_rows, epoch_times, trial_rates))

    in_specs = (
        P("epoch", "row", None),
        P("epoch", "row", None),
        P("epoch", "row", None),
        P("epoch", None),
        P("epoch", None),
        P("epoch"),
        P(),
    )
    out_specs = (P("epoch", "row", None), P("epoch", "row", None))
    return jax.shard_map(
        on_device, mesh=mesh, in_specs=in_specs, out_specs=out_specs, check_vma=False
    )
```

```python
import functools

import jax
import jax.numpy as jnp
from jax import lax
from jax.experimental import pallas as pl
from jax.experimental.pallas import tpu as pltpu
from jax.sharding import PartitionSpec as P

HALO = 8
PAD = 6
TSPAN = 64
TAPS = 2 * PAD + 1
LANES = 128
NEAR = 8
OVER = 3 * NEAR
BAND = 2 * LANES
TALL = BAND + 2 * HALO
MESH = pl.DeviceIdType.MESH
F32 = jnp.float32
BF16 = jnp.bfloat16


def split(x):
    high = x.astype(BF16)
    return high, (x - high.astype(F32)).astype(BF16)


def iota(shape, axis):
    return lax.broadcasted_iota(jnp.int32, shape, axis)


def kernel(
    sizes,
    flux_hbm, inv_hbm, mask_hbm, psf_columns, psf_rows, times, rates,
    out_psi, out_phi,
    flux, inv, mask, toeplitz, padded, shifted,
    pair_out_over, pair_out_mid, pair_in_over, pair_in_mid,
    own_over, own_mid, far_in_over, far_in_mid,
    up_out, down_out, up_in, down_in,
    load_sem, pair_send, pair_recv, far_send, far_recv, row_send, row_recv,
):
    groups, row_devices = sizes
    epochs, rows, columns = flux.shape
    tiles = columns // LANES
    depth = epochs * rows
    me = lax.axis_index("epoch")
    core, group = lax.rem(me, 2), me // 2
    partner = me + 1 - 2 * core
    row = lax.axis_index("row")
    outs = (out_psi, out_phi)

    loads = []
    for e in range(epochs):
        for n, (src, dst) in enumerate(((inv_hbm, inv), (mask_hbm, mask), (flux_hbm, flux))):
            copy = pltpu.make_async_copy(src.at[e], dst.at[e], load_sem.at[e, n])
            copy.start()
            loads.append(copy)

    barrier = pltpu.get_barrier_semaphore()
    pl.semaphore_signal(barrier, inc=1, device_id={"epoch": partner}, device_id_type=MESH)
    for d in range(1, groups):
        there = 2 * lax.rem(group + d, groups) + core
        pl.semaphore_signal(barrier, inc=1, device_id={"epoch": there}, device_id_type=MESH)

    @pl.when(row > 0)
    def _():
        pl.semaphore_signal(barrier, inc=1, device_id={"row": row - 1}, device_id_type=MESH)

    @pl.when(row < row_devices - 1)
    def _():
        pl.semaphore_signal(barrier, inc=1, device_id={"row": row + 1}, device_id_type=MESH)

    offset = BAND // 4 - PAD + HALO
    lane = iota((NEAR, LANES), 1)
    place = iota((NEAR, LANES), 0) - lane
    wrapped = lax.rem(place - offset + 4 * LANES, LANES)
    for e in range(epochs):
        plain = jnp.zeros((NEAR, LANES), F32)
        for tap in range(TAPS):
            plain = jnp.where(wrapped == tap, psf_columns[e, tap], plain)
        for m in range(TALL // NEAR):
            turned = pltpu.roll(plain, (NEAR * m) % LANES, 1) if (NEAR * m) % LANES else plain
            where = place + (NEAR * m - offset)
            turned = jnp.where((where >= 0) & (where < TAPS), turned, 0.0)
            toeplitz[e, 0, m * NEAR : (m + 1) * NEAR, :] = turned
            toeplitz[e, 1, m * NEAR : (m + 1) * NEAR, :] = turned * turned

    half_lane = iota((rows, LANES), 1) < LANES // 2
    for e in range(epochs):
        for copy in loads[3 * e : 3 * e + 3]:
            copy.wait()
        weights = inv[e] * mask[e].astype(F32)
        for f, field in enumerate((flux[e] * weights, weights)):
            turned = pltpu.roll(field, LANES // 2, 1)
            first = turned[:, :LANES]
            for n, piece in enumerate(split(turned)):
                padded[e, f, n, :, LANES:columns] = piece[:, LANES:]
            for n, piece in enumerate(split(jnp.where(half_lane, 0.0, first))):
                padded[e, f, n, :, :LANES] = piece
            for n, piece in enumerate(split(jnp.where(half_lane, first, 0.0))):
                padded[e, f, n, :, columns:] = piece

    def shift(v, axis, e):
        return (rates[axis, v] * times[e]) >> (TSPAN.bit_length() - 1)

    def row_matrices(v):
        shape = (OVER + rows + NEAR, depth)
        o, k = iota(shape, 0), iota(shape, 1)
        far = jnp.where(rates[0, v] >= 0, -2 * NEAR, rows + NEAR)
        r = jnp.where(o < NEAR, o - NEAR, rows + o - NEAR)
        r = jnp.where(o >= 2 * NEAR, o - 2 * NEAR + far, r)
        r = jnp.where(o >= OVER, o - OVER, r)
        epoch_of = k // rows
        step = jnp.zeros(shape, jnp.int32)
        for e in range(epochs):
            step = jnp.where(epoch_of == e, shift(v, 0, e), step)
        at = r + step
        good = (at + row * rows >= 0) & (at + row * rows < rows * row_devices) & (o < OVER + rows)
        tap_at = jnp.where(good, lax.rem(k, rows) - at + PAD, -1)
        one_row = epoch_of[:1]
        plain = jnp.zeros(shape, F32)
        for tap in range(TAPS):
            value = jnp.zeros((1, depth), F32)
            for e in range(epochs):
                value = jnp.where(one_row == e, psf_rows[e, tap], value)
            plain = jnp.where(tap_at == tap, value, plain)
        return split(plain), split(plain * plain)

    def columns_stage(pair, f):
        lanes = iota((rows, 2 * LANES), 1)
        for e in range(epochs):
            steps = [shift(v, 1, e) for v in pair]
            band = jnp.concatenate(
                [toeplitz[e, f, pl.ds(HALO - s, BAND), :] for s in steps], axis=1
            )
            band_high, band_low = split(band)
            high, low = (
                jnp.concatenate(
                    [padded[e, f, n, :, t * LANES : t * LANES + BAND] for t in range(tiles)], axis=0
                )
                for n in range(2)
            )
            result = jnp.dot(
                jnp.concatenate([high, low, high], axis=1),
                jnp.concatenate([band_high, band_high, band_low], axis=0),
                preferred_element_type=F32,
            )
            source = lax.rem(lanes, LANES) + jnp.where(lanes < LANES, steps[0], steps[1])
            for t in range(tiles):
                block = result[t * rows : (t + 1) * rows]
                if t == 0:
                    block = jnp.where(source >= 0, block, 0.0)
                if t == tiles - 1:
                    block = jnp.where(source + t * LANES < columns, block, 0.0)
                high_block, low_block = split(block)
                for h in range(2):
                    at = slice(t * LANES, (t + 1) * LANES)
                    part = slice(h * LANES, (h + 1) * LANES)
                    shifted[h, e * rows : (e + 1) * rows, at] = high_block[:, part]
                    shifted[h, depth + e * rows : depth + (e + 1) * rows, at] = low_block[:, part]

    def rows_stage(h, matrix):
        high, low = matrix
        return jnp.dot(
            jnp.concatenate([high, high], axis=1), shifted[h], preferred_element_type=F32
        ) + jnp.dot(low, shifted[h, :depth], preferred_element_type=F32)

    def pair_copy(d, f, part):
        src, dst = ((pair_out_over, pair_in_over), (pair_out_mid, pair_in_mid))[part]
        return pltpu.make_async_remote_copy(
            src_ref=src.at[d, f], dst_ref=dst.at[d, f],
            send_sem=pair_send.at[d, f, part], recv_sem=pair_recv.at[d, f, part],
            device_id={"epoch": partner}, device_id_type=MESH,
        )

    def far_copy(d, f, part):
        src, dst = ((own_over, far_in_over), (own_mid, far_in_mid))[part]
        return pltpu.make_async_remote_copy(
            src_ref=src.at[d, f], dst_ref=dst.at[d - 1, f],
            send_sem=far_send.at[d - 1, f, part], recv_sem=far_recv.at[d - 1, f, part],
            device_id={"epoch": 2 * lax.rem(group + d, groups) + core}, device_id_type=MESH,
        )

    def row_copy(f, way, other):
        src, dst = ((up_out, down_in), (down_out, up_in))[way]
        return pltpu.make_async_remote_copy(
            src_ref=src.at[f], dst_ref=dst.at[f],
            send_sem=row_send.at[f, way], recv_sem=row_recv.at[f, way],
            device_id={"row": other}, device_id_type=MESH,
        )

    def finish(d, f):
        for part, (own, arrived) in enumerate(((own_over, pair_in_over), (own_mid, pair_in_mid))):
            pair_copy(d, f, part).wait_recv()
            own[d, f] = own[d, f] + arrived[d, f]
            if d:
                far_copy(d, f, part).start()

    order = list(range(1, groups)) + [0]
    before = None
    for d in order:
        goal = 2 * lax.rem(group + d, groups)
        pair = (goal + 1 - core, goal + core)
        matrices = [row_matrices(v) for v in pair]
        for f in range(2):
            columns_stage(pair, f)
            if before is None:
                above = lax.div(row + row_devices - 1, row_devices)
                below = lax.div(2 * row_devices - 2 - row, row_devices)
                pl.semaphore_wait(barrier, groups + above + below)
            else:
                finish(*before)
            part = rows_stage(0, matrices[0][f])
            pair_out_over[d, f] = part[:OVER]
            pair_out_mid[d, f] = part[OVER : OVER + rows]
            pair_copy(d, f, 0).start()
            pair_copy(d, f, 1).start()
            part = rows_stage(1, matrices[1][f])
            own_over[d, f] = part[:OVER]
            own_mid[d, f] = part[OVER : OVER + rows]
            before = (d, f)
    finish(*before)

    upward = rates[0, me] >= 0
    for f in range(2):
        total = own_over[0, f]
        for d in range(1, groups):
            far_copy(d, f, 0).wait_recv()
            total = total + far_in_over[d - 1, f]
        far = total[2 * NEAR :]
        up_out[f, :NEAR] = jnp.where(upward, far, 0.0)
        up_out[f, NEAR:] = total[:NEAR]
        down_out[f, :NEAR] = total[NEAR : 2 * NEAR]
        down_out[f, NEAR:] = jnp.where(upward, 0.0, far)

        @pl.when(row > 0)
        def _():
            row_copy(f, 0, row - 1).start()

        @pl.when(row < row_devices - 1)
        def _():
            row_copy(f, 1, row + 1).start()

        total = own_mid[0, f]
        for d in range(1, groups):
            far_copy(d, f, 1).wait_recv()
            total = total + far_in_mid[d - 1, f]
        outs[f][0] = total

    for f in range(2):
        @pl.when(row > 0)
        def _():
            row_copy(f, 1, row - 1).wait_recv()
            outs[f][0, : 2 * NEAR] = outs[f][0, : 2 * NEAR] + up_in[f]

        @pl.when(row < row_devices - 1)
        def _():
            row_copy(f, 0, row + 1).wait_recv()
            outs[f][0, rows - 2 * NEAR :] = outs[f][0, rows - 2 * NEAR :] + down_in[f]

    for f in range(2):
        for part in range(2):
            for d in range(groups):
                pair_copy(d, f, part).wait_send()
            for d in range(1, groups):
                far_copy(d, f, part).wait_send()

        @pl.when(row > 0)
        def _():
            row_copy(f, 0, row - 1).wait_send()

        @pl.when(row < row_devices - 1)
        def _():
            row_copy(f, 1, row + 1).wait_send()


def solution(mesh):
    epoch_devices, row_devices = mesh.shape["epoch"], mesh.shape["row"]
    groups = epoch_devices // 2

    def on_device(flux_image, inv_var, pixel_mask, psf_columns, psf_rows, epoch_times, trial_rates):
        epochs, rows, columns = flux_image.shape
        depth = epochs * rows
        assert epoch_devices % 2 == 0 and trial_rates.shape[0] == epoch_devices
        assert rows % (2 * NEAR) == 0 and columns % LANES == 0 and depth % LANES == 0
        far = max(groups - 1, 1)
        hbm = pl.BlockSpec(memory_space=pl.ANY)
        smem = pl.BlockSpec(memory_space=pltpu.SMEM)
        vmem = pl.BlockSpec(memory_space=pltpu.VMEM)
        image = (epochs, rows, columns)

        def pieces(count):
            return [
                pltpu.VMEM((count, 2, OVER, columns), F32),
                pltpu.VMEM((count, 2, rows, columns), F32),
            ]

        edge = pltpu.VMEM((2, 2 * NEAR, columns), F32)
        dma = pltpu.SemaphoreType.DMA
        return tuple(pl.pallas_call(
            functools.partial(kernel, (groups, row_devices)),
            out_shape=[pltpu.VMEM((1, rows, columns), F32)] * 2,
            in_specs=[hbm] * 3 + [smem] * 4,
            out_specs=[vmem] * 2,
            scratch_shapes=[
                pltpu.VMEM(image, F32),
                pltpu.VMEM(image, F32),
                pltpu.VMEM(image, jnp.int32),
                pltpu.VMEM((epochs, 2, TALL, LANES), F32),
                pltpu.VMEM((epochs, 2, 2, rows, columns + LANES), BF16),
                pltpu.VMEM((2, 2 * depth, columns), BF16),
                *pieces(groups),
                *pieces(groups),
                *pieces(groups),
                *pieces(far),
                edge, edge, edge, edge,
                dma((epochs, 3)),
                dma((groups, 2, 2)),
                dma((groups, 2, 2)),
                dma((far, 2, 2)),
                dma((far, 2, 2)),
                dma((2, 2)),
                dma((2, 2)),
            ],
            compiler_params=pltpu.CompilerParams(collective_id=0, has_side_effects=True),
        )(flux_image, inv_var, pixel_mask, psf_columns, psf_rows, epoch_times, trial_rates.T))

    in_specs = (
        P("epoch", "row", None),
        P("epoch", "row", None),
        P("epoch", "row", None),
        P("epoch", None),
        P("epoch", None),
        P("epoch"),
        P(),
    )
    out_specs = (P("epoch", "row", None), P("epoch", "row", None))
    return jax.shard_map(
        on_device, mesh=mesh, in_specs=in_specs, out_specs=out_specs, check_vma=False
    )
```

```python
import functools

import jax
import jax.numpy as jnp
from jax import lax
from jax.experimental import pallas as pl
from jax.experimental.pallas import tpu as pltpu
from jax.sharding import PartitionSpec as P

HALO = 8
PAD = 6
TSPAN = 64
TAPS = 2 * PAD + 1
LANES = 128
NEAR = 8
OVER = 3 * NEAR
BAND = 2 * LANES
TALL = BAND + 2 * HALO
MESH = pl.DeviceIdType.MESH
F32 = jnp.float32
BF16 = jnp.bfloat16


def split(x):
    high = x.astype(BF16)
    return high, (x - high.astype(F32)).astype(BF16)


def iota(shape, axis):
    return lax.broadcasted_iota(jnp.int32, shape, axis)


def kernel(
    sizes,
    flux_hbm, inv_hbm, mask_hbm, psf_columns, psf_rows, times, rates,
    out_psi, out_phi,
    flux, inv, mask, toeplitz, padded, shifted,
    pair_out_over, pair_out_mid, pair_in_over, pair_in_mid,
    own_over, own_mid, far_in_over, far_in_mid,
    up_out, down_out, up_in, down_in,
    load_sem, pair_send, pair_recv, far_send, far_recv, row_send, row_recv,
):
    groups, row_devices = sizes
    epochs, rows, columns = flux.shape
    tiles = columns // LANES
    depth = epochs * rows
    me = lax.axis_index("epoch")
    core, group = lax.rem(me, 2), me // 2
    partner = me + 1 - 2 * core
    row = lax.axis_index("row")
    outs = (out_psi, out_phi)

    loads = []
    for e in range(epochs):
        for n, (src, dst) in enumerate(((inv_hbm, inv), (mask_hbm, mask), (flux_hbm, flux))):
            copy = pltpu.make_async_copy(src.at[e], dst.at[e], load_sem.at[e, n])
            copy.start()
            loads.append(copy)

    barrier = pltpu.get_barrier_semaphore()
    pl.semaphore_signal(barrier, inc=1, device_id={"epoch": partner}, device_id_type=MESH)
    for d in range(1, groups):
        there = 2 * lax.rem(group + d, groups) + core
        pl.semaphore_signal(barrier, inc=1, device_id={"epoch": there}, device_id_type=MESH)

    @pl.when(row > 0)
    def _():
        pl.semaphore_signal(barrier, inc=1, device_id={"row": row - 1}, device_id_type=MESH)

    @pl.when(row < row_devices - 1)
    def _():
        pl.semaphore_signal(barrier, inc=1, device_id={"row": row + 1}, device_id_type=MESH)

    offset = BAND // 4 - PAD + HALO
    lane = iota((NEAR, LANES), 1)
    place = iota((NEAR, LANES), 0) - lane
    wrapped = lax.rem(place - offset + 4 * LANES, LANES)
    for e in range(epochs):
        plain = jnp.zeros((NEAR, LANES), F32)
        for tap in range(TAPS):
            plain = jnp.where(wrapped == tap, psf_columns[e, tap], plain)
        for m in range(TALL // NEAR):
            turned = pltpu.roll(plain, (NEAR * m) % LANES, 1) if (NEAR * m) % LANES else plain
            where = place + (NEAR * m - offset)
            turned = jnp.where((where >= 0) & (where < TAPS), turned, 0.0)
            toeplitz[e, 0, m * NEAR : (m + 1) * NEAR, :] = turned
            toeplitz[e, 1, m * NEAR : (m + 1) * NEAR, :] = turned * turned

    half_lane = iota((rows, LANES), 1) < LANES // 2
    for e in range(epochs):
        for copy in loads[3 * e : 3 * e + 3]:
            copy.wait()
        weights = inv[e] * mask[e].astype(F32)
        for f, field in enumerate((flux[e] * weights, weights)):
            turned = pltpu.roll(field, LANES // 2, 1)
            first = turned[:, :LANES]
            for n, piece in enumerate(split(turned)):
                padded[e, f, n, :, LANES:columns] = piece[:, LANES:]
            for n, piece in enumerate(split(jnp.where(half_lane, 0.0, first))):
                padded[e, f, n, :, :LANES] = piece
            for n, piece in enumerate(split(jnp.where(half_lane, first, 0.0))):
                padded[e, f, n, :, columns:] = piece

    def shift(v, axis, e):
        return (rates[axis, v] * times[e]) >> (TSPAN.bit_length() - 1)

    def row_matrices(v):
        shape = (OVER + rows + NEAR, depth)
        o, k = iota(shape, 0), iota(shape, 1)
        far = jnp.where(rates[0, v] >= 0, -2 * NEAR, rows + NEAR)
        r = jnp.where(o < NEAR, o - NEAR, rows + o - NEAR)
        r = jnp.where(o >= 2 * NEAR, o - 2 * NEAR + far, r)
        r = jnp.where(o >= OVER, o - OVER, r)
        epoch_of = k // rows
        step = jnp.zeros(shape, jnp.int32)
        for e in range(epochs):
            step = jnp.where(epoch_of == e, shift(v, 0, e), step)
        at = r + step
        good = (at + row * rows >= 0) & (at + row * rows < rows * row_devices) & (o < OVER + rows)
        tap_at = jnp.where(good, lax.rem(k, rows) - at + PAD, -1)
        one_row = epoch_of[:1]
        plain = jnp.zeros(shape, F32)
        for tap in range(TAPS):
            value = jnp.zeros((1, depth), F32)
            for e in range(epochs):
                value = jnp.where(one_row == e, psf_rows[e, tap], value)
            plain = jnp.where(tap_at == tap, value, plain)
        return split(plain), split(plain * plain)

    def columns_stage(pair, f):
        lanes = iota((rows, 2 * LANES), 1)
        for e in range(epochs):
            steps = [shift(v, 1, e) for v in pair]
            band = jnp.concatenate(
                [toeplitz[e, f, pl.ds(HALO - s, BAND), :] for s in steps], axis=1
            )
            band_high, band_low = split(band)
            high, low = (
                jnp.concatenate(
                    [padded[e, f, n, :, t * LANES : t * LANES + BAND] for t in range(tiles)], axis=0
                )
                for n in range(2)
            )
            result = jnp.dot(
                jnp.concatenate([high, low, high], axis=1),
                jnp.concatenate([band_high, band_high, band_low], axis=0),
                preferred_element_type=F32,
            )
            source = lax.rem(lanes, LANES) + jnp.where(lanes < LANES, steps[0], steps[1])
            for t in range(tiles):
                block = result[t * rows : (t + 1) * rows]
                if t == 0:
                    block = jnp.where(source >= 0, block, 0.0)
                if t == tiles - 1:
                    block = jnp.where(source + t * LANES < columns, block, 0.0)
                high_block, low_block = split(block)
                for h in range(2):
                    at = slice(t * LANES, (t + 1) * LANES)
                    part = slice(h * LANES, (h + 1) * LANES)
                    shifted[h, e * rows : (e + 1) * rows, at] = high_block[:, part]
                    shifted[h, depth + e * rows : depth + (e + 1) * rows, at] = low_block[:, part]

    def rows_stage(h, matrix):
        high, low = matrix
        return jnp.dot(
            jnp.concatenate([high, high], axis=1), shifted[h], preferred_element_type=F32
        ) + jnp.dot(low, shifted[h, :depth], preferred_element_type=F32)

    def pair_copy(d, f, part):
        src, dst = ((pair_out_over, pair_in_over), (pair_out_mid, pair_in_mid))[part]
        return pltpu.make_async_remote_copy(
            src_ref=src.at[d, f], dst_ref=dst.at[d, f],
            send_sem=pair_send.at[d, f, part], recv_sem=pair_recv.at[d, f, part],
            device_id={"epoch": partner}, device_id_type=MESH,
        )

    def far_copy(d, f, part):
        src, dst = ((own_over, far_in_over), (own_mid, far_in_mid))[part]
        return pltpu.make_async_remote_copy(
            src_ref=src.at[d, f], dst_ref=dst.at[d - 1, f],
            send_sem=far_send.at[d - 1, f, part], recv_sem=far_recv.at[d - 1, f, part],
            device_id={"epoch": 2 * lax.rem(group + d, groups) + core}, device_id_type=MESH,
        )

    def row_copy(f, way, other):
        src, dst = ((up_out, down_in), (down_out, up_in))[way]
        return pltpu.make_async_remote_copy(
            src_ref=src.at[f], dst_ref=dst.at[f],
            send_sem=row_send.at[f, way], recv_sem=row_recv.at[f, way],
            device_id={"row": other}, device_id_type=MESH,
        )

    def finish(d, f, part):
        own, arrived = ((own_over, pair_in_over), (own_mid, pair_in_mid))[part]
        pair_copy(d, f, part).wait_recv()
        own[d, f] = own[d, f] + arrived[d, f]
        if d:
            far_copy(d, f, part).start()

    order = list(range(1, groups)) + [0]
    waiting = []
    entered = False
    for d in order:
        goal = 2 * lax.rem(group + d, groups)
        pair = (goal + 1 - core, goal + core)
        matrices = [row_matrices(v) for v in pair]
        for f in range(2):
            columns_stage(pair, f)
            if not entered:
                above = lax.div(row + row_devices - 1, row_devices)
                below = lax.div(2 * row_devices - 2 - row, row_devices)
                pl.semaphore_wait(barrier, groups + above + below)
                entered = True
            for n in waiting:
                finish(*n)
            part = rows_stage(0, matrices[0][f])
            pair_out_over[d, f] = part[:OVER]
            pair_copy(d, f, 0).start()
            pair_out_mid[d, f] = part[OVER : OVER + rows]
            pair_copy(d, f, 1).start()
            part = rows_stage(1, matrices[1][f])
            own_over[d, f] = part[:OVER]
            own_mid[d, f] = part[OVER : OVER + rows]
            waiting = [(d, f, 0)] if f == 0 else [(d, 1, 0), (d, 0, 1), (d, 1, 1)]
    for n in waiting[:1]:
        finish(*n)

    upward = rates[0, me] >= 0
    for f in range(2):
        total = own_over[0, f]
        for d in range(1, groups):
            far_copy(d, f, 0).wait_recv()
            total = total + far_in_over[d - 1, f]
        far = total[2 * NEAR :]
        up_out[f, :NEAR] = jnp.where(upward, far, 0.0)
        up_out[f, NEAR:] = total[:NEAR]
        down_out[f, :NEAR] = total[NEAR : 2 * NEAR]
        down_out[f, NEAR:] = jnp.where(upward, 0.0, far)

        @pl.when(row > 0)
        def _():
            row_copy(f, 0, row - 1).start()

        @pl.when(row < row_devices - 1)
        def _():
            row_copy(f, 1, row + 1).start()

    for f in range(2):
        finish(0, f, 1)
        total = own_mid[0, f]
        for d in range(1, groups):
            far_copy(d, f, 1).wait_recv()
            total = total + far_in_mid[d - 1, f]
        outs[f][0] = total

    for f in range(2):
        @pl.when(row > 0)
        def _():
            row_copy(f, 1, row - 1).wait_recv()
            outs[f][0, : 2 * NEAR] = outs[f][0, : 2 * NEAR] + up_in[f]

        @pl.when(row < row_devices - 1)
        def _():
            row_copy(f, 0, row + 1).wait_recv()
            outs[f][0, rows - 2 * NEAR :] = outs[f][0, rows - 2 * NEAR :] + down_in[f]

    for f in range(2):
        for part in range(2):
            for d in range(groups):
                pair_copy(d, f, part).wait_send()
            for d in range(1, groups):
                far_copy(d, f, part).wait_send()

        @pl.when(row > 0)
        def _():
            row_copy(f, 0, row - 1).wait_send()

        @pl.when(row < row_devices - 1)
        def _():
            row_copy(f, 1, row + 1).wait_send()


def solution(mesh):
    epoch_devices, row_devices = mesh.shape["epoch"], mesh.shape["row"]
    groups = epoch_devices // 2

    def on_device(flux_image, inv_var, pixel_mask, psf_columns, psf_rows, epoch_times, trial_rates):
        epochs, rows, columns = flux_image.shape
        depth = epochs * rows
        assert epoch_devices % 2 == 0 and trial_rates.shape[0] == epoch_devices
        assert rows % (2 * NEAR) == 0 and columns % LANES == 0 and depth % LANES == 0
        far = max(groups - 1, 1)
        hbm = pl.BlockSpec(memory_space=pl.ANY)
        smem = pl.BlockSpec(memory_space=pltpu.SMEM)
        vmem = pl.BlockSpec(memory_space=pltpu.VMEM)
        image = (epochs, rows, columns)

        def pieces(count):
            return [
                pltpu.VMEM((count, 2, OVER, columns), F32),
                pltpu.VMEM((count, 2, rows, columns), F32),
            ]

        edge = pltpu.VMEM((2, 2 * NEAR, columns), F32)
        dma = pltpu.SemaphoreType.DMA
        return tuple(pl.pallas_call(
            functools.partial(kernel, (groups, row_devices)),
            out_shape=[pltpu.VMEM((1, rows, columns), F32)] * 2,
            in_specs=[hbm] * 3 + [smem] * 4,
            out_specs=[vmem] * 2,
            scratch_shapes=[
                pltpu.VMEM(image, F32),
                pltpu.VMEM(image, F32),
                pltpu.VMEM(image, jnp.int32),
                pltpu.VMEM((epochs, 2, TALL, LANES), F32),
                pltpu.VMEM((epochs, 2, 2, rows, columns + LANES), BF16),
                pltpu.VMEM((2, 2 * depth, columns), BF16),
                *pieces(groups),
                *pieces(groups),
                *pieces(groups),
                *pieces(far),
                edge, edge, edge, edge,
                dma((epochs, 3)),
                dma((groups, 2, 2)),
                dma((groups, 2, 2)),
                dma((far, 2, 2)),
                dma((far, 2, 2)),
                dma((2, 2)),
                dma((2, 2)),
            ],
            compiler_params=pltpu.CompilerParams(collective_id=0, has_side_effects=True),
        )(flux_image, inv_var, pixel_mask, psf_columns, psf_rows, epoch_times, trial_rates.T))

    in_specs = (
        P("epoch", "row", None),
        P("epoch", "row", None),
        P("epoch", "row", None),
        P("epoch", None),
        P("epoch", None),
        P("epoch"),
        P(),
    )
    out_specs = (P("epoch", "row", None), P("epoch", "row", None))
    return jax.shard_map(
        on_device, mesh=mesh, in_specs=in_specs, out_specs=out_specs, check_vma=False
    )
```
